32 devices in a mesh: rows: 8 (over z, y), feat: 4 (over x, core).
Axes of the slice: x: 2, y: 2, z: 4, core: 2. Of those that a mesh axis runs over, the one named last changes fastest.
Arguments:
- codes: int32 [16384, 512], P('rows', 'feat'), may hold values from 0 to 31
- node_ids: int32 [16384], P('rows'), may hold values from 0 to 7
- bag: int32 [16384], P('rows'), may hold values from 0 to 3
- response: bfloat16 [16384], P('rows'), may hold values from -6 to 6
- owner_slot: int32 [8], replicated, may hold values from 0 to 7, each once
- chosen_feature: int32 [8], replicated, may hold values from 0 to 511
- chosen_bin: int32 [8], replicated, may hold values from 0 to 30
Outputs:
- gains: float32 [8, 16384], P('rows', 'feat')
- best_gain: float32 [8], P('rows')
- child_ids: int32 [16384], P('rows')
The draws below stay inside these ranges and needn't reach their ends.
All inputs are finite; a program needn't handle non-finite values.
Results may differ from the reference program's by a relative error of at most 0.0003.
Values sent between devices are 32-bit elements; how exact they have to be, the bound alone decides.
No kernel may reach another device: no remote copies, remote signals or barrier semaphores. Data moves between devices by JAX's collectives and lax.ppermute only.
A program may use at most 64 MiB of HBM per device.

```python
import math
import jax
import jax.numpy as jnp
import numpy as np
from jax import lax

FEAT = 512
BINS = 32
NODES = 8
ROWS = 16384


def with_ends(array, stream_key, low, largest):
    place = [jax.random.randint(jax.random.fold_in(stream_key, axis), (), 0, length) for axis, length in enumerate(array.shape)]
    main_axis = array.shape.index(max(array.shape))
    beside = place[:main_axis] + [(place[main_axis] + 1) % array.shape[main_axis]] + place[main_axis + 1:]
    return array.at[tuple(place)].set(low).at[tuple(beside)].set(largest)


def level_of(key, dims, shards, smallest, top_value):
    gain, own = 1.0, jax.random.fold_in(key, 6)
    for axis_at, shards_of in shards:
        heights = jnp.exp(jax.random.uniform(jax.random.fold_in(own, axis_at), (shards_of,), jnp.float32, smallest / len(shards), top_value / len(shards)))
        gain = gain * jnp.repeat(heights, dims[axis_at] // shards_of).reshape([-1 if axis == axis_at else 1 for axis in range(len(dims))])
    return gain


def cumulative_ranks(amount, slope):
    loads = [(1 << 20) // math.isqrt(standing ** slope) + 1 for standing in range(1, amount + 1)]
    scale = 1 + sum(loads) // (1 << 30)
    return np.cumsum(np.array([max(1, weight // scale) for weight in loads]))


def skewed_ids(rng, dims, count, lean):
    grid = cumulative_ranks(count, lean)
    ticket = jax.random.randint(jax.random.fold_in(rng, 1), dims, 0, int(grid[count - 1]))
    standing = jnp.searchsorted(jnp.asarray(grid, jnp.int32), ticket, side="right")
    return jax.random.permutation(jax.random.fold_in(rng, 2), count)[standing].astype(jnp.int32)


def gaussian(stream_key, extent, scale, most, split=(), kind=jnp.bfloat16):
    values = scale * jax.random.normal(stream_key, extent, jnp.float32)
    if split:
        values = values * level_of(stream_key, extent, split, -0.22, 0.18)
    return jnp.clip(values, -most, most).astype(kind)


def setup_inputs(seed: int = 0) -> dict:
    streams_of = jax.random.split(jax.random.key(seed), 8)
    return {
        "codes": with_ends(jax.random.randint(streams_of[0], (ROWS, FEAT), 0, BINS), jax.random.fold_in(streams_of[0], 1), 0, BINS - 1).astype(jnp.int32),
        "node_ids": with_ends(skewed_ids(streams_of[1], (ROWS,), NODES, 2), jax.random.fold_in(streams_of[1], 3), 0, NODES - 1).astype(jnp.int32),
        "bag": with_ends(jax.random.randint(streams_of[2], (ROWS,), 0, 4), jax.random.fold_in(streams_of[2], 1), 0, 3).astype(jnp.int32),
        "response": gaussian(streams_of[3], (ROWS,), 1.0, 6.0, ((0, 8),)),
        "owner_slot": jax.random.permutation(streams_of[4], NODES).astype(jnp.int32),
        "chosen_feature": with_ends(jax.random.randint(streams_of[5], (NODES,), 0, FEAT), jax.random.fold_in(streams_of[5], 1), 0, FEAT - 1).astype(jnp.int32),
        "chosen_bin": with_ends(jax.random.randint(streams_of[6], (NODES,), 0, BINS - 1), jax.random.fold_in(streams_of[6], 1), 0, (BINS - 1) - 1).astype(jnp.int32),
    }


LAMBDA = 1.0


def reference(codes, node_ids, bag, response, owner_slot, chosen_feature, chosen_bin):
    weight = bag.astype(jnp.float32)
    grad = weight * response.astype(jnp.float32)
    slot = owner_slot[node_ids]
    block = 64
    count = codes.shape[0]

    def per_block(index):
        piece = lax.dynamic_slice_in_dim(codes, (index * block).astype(jnp.int32), block, 1)
        seg = slot[:, None] * (block * BINS) + jnp.arange(block, dtype=jnp.int32)[None, :] * BINS + piece
        seg = seg.reshape(-1)
        hw = jax.ops.segment_sum(jnp.broadcast_to(weight[:, None], (count, block)).reshape(-1), seg, NODES * block * BINS)
        hg = jax.ops.segment_sum(jnp.broadcast_to(grad[:, None], (count, block)).reshape(-1), seg, NODES * block * BINS)
        return jnp.stack([hw.reshape(NODES, block * BINS), hg.reshape(NODES, block * BINS)])

    stacked = lax.map(per_block, jnp.arange(FEAT // block, dtype=jnp.int32))
    stacked = stacked.transpose(1, 2, 0, 3).reshape(2, NODES, FEAT, BINS)
    hist_w, hist_g = stacked[0], stacked[1]
    left_w = jnp.cumsum(hist_w, axis=2)
    left_g = jnp.cumsum(hist_g, axis=2)
    total_w = jnp.sum(hist_w, axis=2, keepdims=True)
    total_g = jnp.sum(hist_g, axis=2, keepdims=True)
    right_w = total_w - left_w
    right_g = total_g - left_g
    gains = left_g * left_g / (left_w + LAMBDA) + right_g * right_g / (right_w + LAMBDA) - total_g * total_g / (total_w + LAMBDA)
    gains = gains.reshape(NODES, FEAT * BINS)
    best_gain = jnp.max(gains, axis=1)
    feat_row = chosen_feature[node_ids]
    code = jnp.take_along_axis(codes, feat_row[:, None], axis=1)[:, 0]
    right = (code > chosen_bin[node_ids]).astype(jnp.int32)
    child_ids = 2 * node_ids + right
    return gains, best_gain, child_ids
```

```python
import functools

import jax
import jax.numpy as jnp
from jax import lax
from jax.experimental import pallas as pl
from jax.experimental.pallas import tpu as pltpu
from jax.sharding import PartitionSpec as P

BINS = 32
LAMBDA = 1.0
LANES = 128
F8 = jnp.float8_e4m3fn
VMEM = pl.BlockSpec(memory_space=pltpu.VMEM)
HBM = pl.BlockSpec(memory_space=pltpu.HBM)
SMEM = pl.BlockSpec(memory_space=pltpu.SMEM)

DIGITS = 10
PARTS = 4
SMALL = 4


def power_of_two_scale(top):
    top = top * 2.0**-4
    scale, inverse = jnp.full_like(top, 2.0**-4), jnp.full_like(top, 2.0**4)
    for step in (64, 32, 16, 8, 4, 2, 1):
        low = top < 2.0 ** (1 - step)
        top = jnp.where(low, top * 2.0**step, top)
        scale = jnp.where(low, scale * 2.0**step, scale)
        inverse = jnp.where(low, inverse * 2.0**-step, inverse)
    return scale, inverse


def digits_of(value):
    magic = 1.5 * 2.0**23
    digits = []
    for _ in range(DIGITS):
        digit = (value + magic) - magic
        digits.append(digit)
        value = (value - digit) * 4.0
    return digits


def place_of(row, owned, ranks):
    bits = ranks.bit_length() - 1
    far = lax.shift_right_logical(row, jnp.full_like(row, owned.bit_length() - 1))
    place = row & (owned - 1)
    for turn in range(bits):
        bit = lax.shift_right_logical(far, jnp.full_like(far, bits - 1 - turn)) & 1
        place = place + bit * (owned << turn)
    return place


def hist_kernel(
    owned, owner_hbm, codes_hbm, node_hbm, bag_hbm, resp_hbm,
    keep_ref, send_ref, code_ref, node_ref, owner_ref, codes_ref, bag_ref, resp_ref, sems,
):
    nodes = owner_ref.shape[0]
    chunks = node_ref.shape[0]
    rows, feat = codes_ref.shape
    part = rows // PARTS
    copies = [
        pltpu.make_async_copy(node_hbm, node_ref, sems.at[0]),
        pltpu.make_async_copy(bag_hbm, bag_ref, sems.at[1]),
        pltpu.make_async_copy(resp_hbm, resp_ref, sems.at[2]),
        pltpu.make_async_copy(owner_hbm, owner_ref, sems.at[3]),
    ]
    for p in range(PARTS):
        span = pl.ds(p * part, part)
        copies.append(pltpu.make_async_copy(codes_hbm.at[span], codes_ref.at[span], sems.at[SMALL + p]))
    for copy in copies:
        copy.start()
    for copy in copies[:SMALL]:
        copy.wait()
    mine = lax.axis_index("rows") * owned
    node = node_ref[...]
    slot = jnp.zeros_like(node)
    for n in range(nodes):
        slot = jnp.where(node == n, owner_ref[n], slot)
    slot = slot ^ mine
    bag = bag_ref[...]
    weight = bag.astype(jnp.float32)
    grad = weight * resp_ref[...].astype(jnp.float32)
    top = jnp.max(jnp.max(jnp.abs(grad), axis=1, keepdims=True), axis=0, keepdims=True)
    scale, inverse = power_of_two_scale(top)
    values = [(bag & 1).astype(jnp.float32), (bag >> 1).astype(jnp.float32)] + digits_of(grad * scale)
    row = place_of(lax.broadcasted_iota(jnp.int32, (nodes, LANES), 0), owned, nodes // owned)
    columns = []
    for i in range(chunks):
        hit = slot[i : i + 1, :] == row
        picked = [jnp.where(hit, v[i : i + 1, :], 0.0) for v in values]
        columns.append(jnp.concatenate(picked, axis=0).astype(F8))
    picks = jnp.concatenate(columns, axis=1)
    for p in range(PARTS):
        copies[SMALL + p].wait()
        code_ref[p * part : (p + 1) * part, :] = codes_ref[p * part : (p + 1) * part, :].astype(jnp.int8)
    one, zero = jnp.asarray(1, F8), jnp.asarray(0, F8)
    for b in range(0, BINS, 2):
        code = code_ref[...]
        masks = [jnp.where(code <= jnp.asarray(b + j, jnp.int8), one, zero) for j in range(2)]
        sums = jnp.dot(picks, jnp.concatenate(masks, axis=1), preferred_element_type=jnp.float32)
        bags = sums[:nodes] + 2.0 * sums[nodes : 2 * nodes]
        grads = sums[(DIGITS + 1) * nodes :]
        for d in range(DIGITS, 1, -1):
            grads = grads * 0.25 + sums[d * nodes : (d + 1) * nodes]
        grads = grads * inverse
        for j in range(2):
            for at, table in ((b + j, bags), (BINS + b + j, grads)):
                piece = table[:, j * feat : (j + 1) * feat]
                keep_ref[:, at, :] = piece[: nodes // 2]
                send_ref[:, at, :] = piece[nodes // 2 :]


def flags_kernel(feature_ref, bin_ref, codes_ref, node_ref, out_ref):
    nodes = feature_ref.shape[0]
    chunks = node_ref.shape[0]
    feat = codes_ref.shape[1]
    base = lax.axis_index("feat") * feat
    lane = lax.broadcasted_iota(jnp.int32, (nodes, feat), 1)
    row = lax.broadcasted_iota(jnp.int32, (nodes, feat), 0)
    want = jnp.zeros((nodes, feat), jnp.int32)
    for n in range(nodes):
        want = jnp.where(row == n, feature_ref[n] - base, want)
    choose = (want == lane).astype(jnp.float32).astype(jnp.bfloat16)
    codes = codes_ref[...].astype(jnp.bfloat16)
    code = lax.dot_general(choose, codes, (((1,), (1,)), ((), ())), preferred_element_type=jnp.float32)
    row = lax.broadcasted_iota(jnp.int32, (nodes, LANES), 0)
    limit = jnp.zeros((nodes, LANES), jnp.int32)
    for n in range(nodes):
        limit = jnp.where(row == n, bin_ref[n], limit)
    limit = limit.astype(jnp.float32)
    for i in range(chunks):
        hit = (node_ref[i : i + 1, :] == row) & (code[:, i * LANES : (i + 1) * LANES] > limit)
        out_ref[i : i + 1, :] = jnp.sum(jnp.where(hit, 1.0, 0.0), axis=0, keepdims=True)


def gains_of(total):
    left_w, left_g = total[:BINS], total[BINS:]
    total_w, total_g = left_w[BINS - 1 :], left_g[BINS - 1 :]
    right_w = total_w - left_w
    right_g = total_g - left_g
    return (
        left_g * left_g / (left_w + LAMBDA)
        + right_g * right_g / (right_w + LAMBDA)
        - total_g * total_g / (total_w + LAMBDA)
    )


def best_kernel(keep_ref, got_ref, flags_ref, out_ref, total_ref):
    chunks = flags_ref.shape[0]
    out_ref[:chunks, :] = flags_ref[...]
    total_ref[...] = keep_ref[...] + got_ref[...]
    for s in range(total_ref.shape[0]):
        gains = gains_of(total_ref[s])
        top = jnp.max(jnp.max(gains, axis=0, keepdims=True), axis=1, keepdims=True)
        out_ref[chunks + s : chunks + s + 1, :] = jnp.broadcast_to(top, (1, LANES))


def gains_kernel(total_ref, out_ref, turn_ref):
    feat = total_ref.shape[2]
    group = LANES // BINS
    for s in range(total_ref.shape[0]):
        turn_ref[...] = gains_of(total_ref[s]).T
        parts = [turn_ref[pl.ds(j, feat // group, stride=group), :] for j in range(group)]
        out_ref[s] = jnp.concatenate(parts, axis=1)


def last_kernel(node_ref, keep_ref, got_ref, best_ref, child_ref):
    chunks = node_ref.shape[0]
    both = jnp.maximum(keep_ref[...], got_ref[...])
    child_ref[...] = 2 * node_ref[...] + (both[:chunks] > 0.5).astype(jnp.int32)
    best_ref[...] = both[chunks : chunks + best_ref.shape[0], :1]


def call(kernel, out, in_specs, out_specs, *args, scratch=(), limit=2):
    return pl.pallas_call(
        kernel,
        out_shape=out,
        in_specs=in_specs,
        out_specs=out_specs,
        scratch_shapes=scratch,
        compiler_params=pltpu.CompilerParams(vmem_limit_bytes=limit << 20),
    )(*args)


def in_hbm(value):
    return pltpu.with_memory_space_constraint(value, pltpu.HBM)


def swap(value, axis, bit):
    return lax.ppermute(value, axis, [(i, i ^ bit) for i in range(lax.axis_size(axis))])


def per_device(codes, node_ids, bag, response, owner_slot, chosen_feature, chosen_bin):
    rows_dev, feat_dev = codes.shape
    nodes = owner_slot.shape[0]
    ranks = lax.axis_size("rows")
    groups = lax.axis_size("feat")
    owned = nodes // ranks
    chunks = rows_dev // LANES
    fold = lambda a: a.reshape(chunks, LANES)
    f32 = lambda *shape: jax.ShapeDtypeStruct(shape, jnp.float32)
    half = f32(nodes // 2, 2 * BINS, feat_dev)
    keep, send, codes, node = call(
        functools.partial(hist_kernel, owned),
        (
            half,
            half,
            jax.ShapeDtypeStruct((rows_dev, feat_dev), jnp.int8),
            jax.ShapeDtypeStruct((chunks, LANES), jnp.int32),
        ),
        [HBM] * 5,
        (VMEM,) * 4,
        *map(in_hbm, (owner_slot, codes, fold(node_ids), fold(bag), fold(response))),
        scratch=[
            pltpu.SMEM((nodes,), jnp.int32),
            pltpu.VMEM((rows_dev, feat_dev), jnp.int32),
            pltpu.VMEM((chunks, LANES), jnp.int32),
            pltpu.VMEM((chunks, LANES), jnp.bfloat16),
            pltpu.SemaphoreType.DMA((SMALL + PARTS,)),
        ],
        limit=6 + nodes // 4,
    )
    got = swap(send, "rows", 1)
    flags = call(
        flags_kernel, f32(chunks, LANES), [SMEM] * 2 + [VMEM] * 2, VMEM,
        chosen_feature, chosen_bin, codes, node, limit=8,
    )
    keep, flags = lax.optimization_barrier((keep, flags))
    for turn in range(1, ranks.bit_length() - 1):
        total = keep + got
        size = total.shape[0] // 2
        keep = total[:size]
        got = swap(total[size:], "rows", 1 << turn)
    pad = -(-owned // 8) * 8
    payload, total = call(
        best_kernel, (f32(chunks + pad, LANES), f32(owned, 2 * BINS, feat_dev)),
        [VMEM] * 3, (VMEM, VMEM), keep, got, flags,
    )
    got = None
    bit = 1
    while bit < groups:
        if got is not None:
            payload = jnp.maximum(payload, got)
        got = swap(payload, "feat", bit)
        bit *= 2
    gains = call(
        gains_kernel, f32(owned, feat_dev * BINS // LANES, LANES), [VMEM], VMEM, total,
        scratch=[pltpu.VMEM((feat_dev, BINS), jnp.float32)],
    )
    best, child = call(
        last_kernel,
        (f32(owned, 1), jax.ShapeDtypeStruct((chunks, LANES), jnp.int32)),
        [VMEM] * 3,
        (VMEM, VMEM),
        node, payload, got,
    )
    return gains.reshape(owned, feat_dev * BINS), best.reshape(owned), child.reshape(rows_dev)


def solution(mesh):
    in_specs = (P("rows", "feat"), P("rows"), P("rows"), P("rows"), P(), P(), P())
    out_specs = (P("rows", "feat"), P("rows"), P("rows"))
    return jax.shard_map(
        per_device, mesh=mesh, in_specs=in_specs, out_specs=out_specs, check_vma=False
    )
```

```python
import functools

import jax
import jax.numpy as jnp
from jax import lax
from jax.experimental import pallas as pl
from jax.experimental.pallas import tpu as pltpu
from jax.sharding import PartitionSpec as P

BINS = 32
LAMBDA = 1.0
LANES = 128
F8 = jnp.float8_e4m3fn
VMEM = pl.BlockSpec(memory_space=pltpu.VMEM)
HBM = pl.BlockSpec(memory_space=pltpu.HBM)
SMEM = pl.BlockSpec(memory_space=pltpu.SMEM)

DIGITS = 10
FIRST, NEXT = 1, 2
ORDER = (1, 2, 3, 4, 5, 6, 7)
FEATS = (1, 2, 3)
PARTS = 4
SMALL = 4


def power_of_two_scale(top):
    top = top * 2.0**-4
    scale, inverse = jnp.full_like(top, 2.0**-4), jnp.full_like(top, 2.0**4)
    for step in (64, 32, 16, 8, 4, 2, 1):
        low = top < 2.0 ** (1 - step)
        top = jnp.where(low, top * 2.0**step, top)
        scale = jnp.where(low, scale * 2.0**step, scale)
        inverse = jnp.where(low, inverse * 2.0**-step, inverse)
    return scale, inverse


def digits_of(value):
    magic = 1.5 * 2.0**23
    digits = []
    for _ in range(DIGITS):
        digit = (value + magic) - magic
        digits.append(digit)
        value = (value - digit) * 4.0
    return digits


def place_of(row, owned, ranks):
    bits = ranks.bit_length() - 1
    far = lax.shift_right_logical(row, jnp.full_like(row, owned.bit_length() - 1))
    place = row & (owned - 1)
    for turn in range(bits):
        bit = lax.shift_right_logical(far, jnp.full_like(far, bits - 1 - turn)) & 1
        place = place + bit * (owned << turn)
    return place


def hist_kernel(
    owned, owner_hbm, codes_hbm, node_hbm, bag_hbm, resp_hbm,
    *refs,
):
    blocks = refs[:-7]
    code_ref, node_ref, owner_ref, codes_ref, bag_ref, resp_ref, sems = refs[-7:]
    nodes = owner_ref.shape[0]
    chunks = node_ref.shape[0]
    rows, feat = codes_ref.shape
    part = rows // PARTS
    copies = [
        pltpu.make_async_copy(node_hbm, node_ref, sems.at[0]),
        pltpu.make_async_copy(bag_hbm, bag_ref, sems.at[1]),
        pltpu.make_async_copy(resp_hbm, resp_ref, sems.at[2]),
        pltpu.make_async_copy(owner_hbm, owner_ref, sems.at[3]),
    ]
    for p in range(PARTS):
        span = pl.ds(p * part, part)
        copies.append(pltpu.make_async_copy(codes_hbm.at[span], codes_ref.at[span], sems.at[SMALL + p]))
    for copy in copies:
        copy.start()
    for copy in copies[:SMALL]:
        copy.wait()
    mine = lax.axis_index("rows") * owned
    node = node_ref[...]
    slot = jnp.zeros_like(node)
    for n in range(nodes):
        slot = jnp.where(node == n, owner_ref[n], slot)
    slot = slot ^ mine
    bag = bag_ref[...]
    weight = bag.astype(jnp.float32)
    grad = weight * resp_ref[...].astype(jnp.float32)
    top = jnp.max(jnp.max(jnp.abs(grad), axis=1, keepdims=True), axis=0, keepdims=True)
    scale, inverse = power_of_two_scale(top)
    values = [(bag & 1).astype(jnp.float32), (bag >> 1).astype(jnp.float32)] + digits_of(grad * scale)
    row = place_of(lax.broadcasted_iota(jnp.int32, (nodes, LANES), 0), owned, nodes // owned)
    columns = []
    for i in range(chunks):
        hit = slot[i : i + 1, :] == row
        picked = [jnp.where(hit, v[i : i + 1, :], 0.0) for v in values]
        columns.append(jnp.concatenate(picked, axis=0).astype(F8))
    picks = jnp.concatenate(columns, axis=1)
    for p in range(PARTS):
        copies[SMALL + p].wait()
        code_ref[p * part : (p + 1) * part, :] = codes_ref[p * part : (p + 1) * part, :].astype(jnp.int8)
    one, zero = jnp.asarray(1, F8), jnp.asarray(0, F8)
    for b in range(0, BINS, 2):
        code = code_ref[...]
        masks = [jnp.where(code <= jnp.asarray(b + j, jnp.int8), one, zero) for j in range(2)]
        sums = jnp.dot(picks, jnp.concatenate(masks, axis=1), preferred_element_type=jnp.float32)
        bags = sums[:nodes] + 2.0 * sums[nodes : 2 * nodes]
        grads = sums[(DIGITS + 1) * nodes :]
        for d in range(DIGITS, 1, -1):
            grads = grads * 0.25 + sums[d * nodes : (d + 1) * nodes]
        grads = grads * inverse
        for j in range(2):
            for at, table in ((b + j, bags), (BINS + b + j, grads)):
                piece = table[:, j * feat : (j + 1) * feat]
                size = nodes // len(blocks)
                for k, block in enumerate(blocks):
                    block[:, at, :] = piece[k * size : (k + 1) * size]


def flags_kernel(feature_ref, bin_ref, codes_ref, node_ref, out_ref):
    nodes = feature_ref.shape[0]
    chunks = node_ref.shape[0]
    feat = codes_ref.shape[1]
    base = lax.axis_index("feat") * feat
    lane = lax.broadcasted_iota(jnp.int32, (nodes, feat), 1)
    row = lax.broadcasted_iota(jnp.int32, (nodes, feat), 0)
    want = jnp.zeros((nodes, feat), jnp.int32)
    for n in range(nodes):
        want = jnp.where(row == n, feature_ref[n] - base, want)
    choose = (want == lane).astype(jnp.float32).astype(jnp.bfloat16)
    codes = codes_ref[...].astype(jnp.bfloat16)
    code = lax.dot_general(choose, codes, (((1,), (1,)), ((), ())), preferred_element_type=jnp.float32)
    row = lax.broadcasted_iota(jnp.int32, (nodes, LANES), 0)
    limit = jnp.zeros((nodes, LANES), jnp.int32)
    for n in range(nodes):
        limit = jnp.where(row == n, bin_ref[n], limit)
    limit = limit.astype(jnp.float32)
    for i in range(chunks):
        hit = (node_ref[i : i + 1, :] == row) & (code[:, i * LANES : (i + 1) * LANES] > limit)
        out_ref[i : i + 1, :] = jnp.sum(jnp.where(hit, 1.0, 0.0), axis=0, keepdims=True)


def gains_of(total):
    left_w, left_g = total[:BINS], total[BINS:]
    total_w, total_g = left_w[BINS - 1 :], left_g[BINS - 1 :]
    right_w = total_w - left_w
    right_g = total_g - left_g
    return (
        left_g * left_g / (left_w + LAMBDA)
        + right_g * right_g / (right_w + LAMBDA)
        - total_g * total_g / (total_w + LAMBDA)
    )


def best_kernel(count, keep_ref, *refs):
    gots, (flags_ref, out_ref, total_ref) = refs[:count], refs[count:]
    chunks = flags_ref.shape[0]
    out_ref[:chunks, :] = flags_ref[...]
    total = keep_ref[...]
    for got in gots:
        total = total + got[...]
    total_ref[...] = total
    for s in range(total_ref.shape[0]):
        gains = gains_of(total_ref[s])
        top = jnp.max(jnp.max(gains, axis=0, keepdims=True), axis=1, keepdims=True)
        out_ref[chunks + s : chunks + s + 1, :] = jnp.broadcast_to(top, (1, LANES))


def gains_kernel(total_ref, out_ref, turn_ref):
    feat = total_ref.shape[2]
    group = LANES // BINS
    for s in range(total_ref.shape[0]):
        turn_ref[...] = gains_of(total_ref[s]).T
        parts = [turn_ref[pl.ds(j, feat // group, stride=group), :] for j in range(group)]
        out_ref[s] = jnp.concatenate(parts, axis=1)


def last_kernel(node_ref, *refs):
    parts, (best_ref, child_ref) = refs[:-2], refs[-2:]
    chunks = node_ref.shape[0]
    both = functools.reduce(jnp.maximum, (part[...] for part in parts))
    child_ref[...] = 2 * node_ref[...] + (both[:chunks] > 0.5).astype(jnp.int32)
    best_ref[...] = both[chunks : chunks + best_ref.shape[0], :1]


def call(kernel, out, in_specs, out_specs, *args, scratch=(), limit=2):
    return pl.pallas_call(
        kernel,
        out_shape=out,
        in_specs=in_specs,
        out_specs=out_specs,
        scratch_shapes=scratch,
        compiler_params=pltpu.CompilerParams(vmem_limit_bytes=limit << 20),
    )(*args)


def in_hbm(value):
    return pltpu.with_memory_space_constraint(value, pltpu.HBM)


def swap(value, axis, distance):
    return lax.ppermute(value, axis, [(i, i ^ distance) for i in range(lax.axis_size(axis))])


def stages_of(ranks):
    bits = ranks.bit_length() - 1
    first = min(FIRST, bits)
    return [range(first)] + [range(t, min(t + NEXT, bits)) for t in range(first, bits, NEXT)]


def exchange(blocks, turns):
    gots = []
    for k in ORDER:
        if k < len(blocks):
            gots.append(swap(blocks[k], "rows", sum(1 << t for t in turns if k >> (turns[-1] - t) & 1)))
    return blocks[0], gots


def per_device(codes, node_ids, bag, response, owner_slot, chosen_feature, chosen_bin):
    rows_dev, feat_dev = codes.shape
    nodes = owner_slot.shape[0]
    ranks = lax.axis_size("rows")
    groups = lax.axis_size("feat")
    owned = nodes // ranks
    chunks = rows_dev // LANES
    fold = lambda a: a.reshape(chunks, LANES)
    f32 = lambda *shape: jax.ShapeDtypeStruct(shape, jnp.float32)
    stages = stages_of(ranks)
    parts = 1 << len(stages[0])
    *blocks, codes, node = call(
        functools.partial(hist_kernel, owned),
        (
            *[f32(nodes // parts, 2 * BINS, feat_dev)] * parts,
            jax.ShapeDtypeStruct((rows_dev, feat_dev), jnp.int8),
            jax.ShapeDtypeStruct((chunks, LANES), jnp.int32),
        ),
        [HBM] * 5,
        (VMEM,) * (2 + parts),
        *map(in_hbm, (owner_slot, codes, fold(node_ids), fold(bag), fold(response))),
        scratch=[
            pltpu.SMEM((nodes,), jnp.int32),
            pltpu.VMEM((rows_dev, feat_dev), jnp.int32),
            pltpu.VMEM((chunks, LANES), jnp.int32),
            pltpu.VMEM((chunks, LANES), jnp.bfloat16),
            pltpu.SemaphoreType.DMA((SMALL + PARTS,)),
        ],
        limit=6 + nodes // 4,
    )
    keep, gots = exchange(blocks, stages[0])
    flags = call(
        flags_kernel, f32(chunks, LANES), [SMEM] * 2 + [VMEM] * 2, VMEM,
        chosen_feature, chosen_bin, codes, node, limit=8,
    )
    keep, flags = lax.optimization_barrier((keep, flags))
    for turns in stages[1:]:
        total = sum(gots, keep)
        size = total.shape[0] >> len(turns)
        keep, gots = exchange([total[k * size : (k + 1) * size] for k in range(1 << len(turns))], turns)
    pad = -(-owned // 8) * 8
    payload, total = call(
        functools.partial(best_kernel, len(gots)),
        (f32(chunks + pad, LANES), f32(owned, 2 * BINS, feat_dev)),
        [VMEM] * (2 + len(gots)), (VMEM, VMEM), keep, *gots, flags,
    )
    parts = [payload]
    for k in FEATS[: groups - 1] + tuple(range(4, groups)):
        parts.append(swap(payload, "feat", k))
    gains = call(
        gains_kernel, f32(owned, feat_dev * BINS // LANES, LANES), [VMEM], VMEM, total,
        scratch=[pltpu.VMEM((feat_dev, BINS), jnp.float32)],
    )
    best, child = call(
        last_kernel,
        (f32(owned, 1), jax.ShapeDtypeStruct((chunks, LANES), jnp.int32)),
        [VMEM] * (1 + groups),
        (VMEM, VMEM),
        node, *parts,
    )
    return gains.reshape(owned, feat_dev * BINS), best.reshape(owned), child.reshape(rows_dev)


def solution(mesh):
    in_specs = (P("rows", "feat"), P("rows"), P("rows"), P("rows"), P(), P(), P())
    out_specs = (P("rows", "feat"), P("rows"), P("rows"))
    return jax.shard_map(
        per_device, mesh=mesh, in_specs=in_specs, out_specs=out_specs, check_vma=False
    )
```

```python
import functools

import jax
import jax.numpy as jnp
from jax import lax
from jax.experimental import pallas as pl
from jax.experimental.pallas import tpu as pltpu
from jax.sharding import PartitionSpec as P

BINS = 32
LAMBDA = 1.0
LANES = 128
F8 = jnp.float8_e4m3fn
VMEM = pl.BlockSpec(memory_space=pltpu.VMEM)
HBM = pl.BlockSpec(memory_space=pltpu.HBM)
SMEM = pl.BlockSpec(memory_space=pltpu.SMEM)

DIGITS = 10
FIRST, NEXT = 2, 1
ORDER = (3, 1, 2)
FEATS = (1, 2, 3)
PARTS = 4
SMALL = 4


def power_of_two_scale(top):
    top = top * 2.0**-4
    scale, inverse = jnp.full_like(top, 2.0**-4), jnp.full_like(top, 2.0**4)
    for step in (64, 32, 16, 8, 4, 2, 1):
        low = top < 2.0 ** (1 - step)
        top = jnp.where(low, top * 2.0**step, top)
        scale = jnp.where(low, scale * 2.0**step, scale)
        inverse = jnp.where(low, inverse * 2.0**-step, inverse)
    return scale, inverse


def digits_of(value):
    magic = 1.5 * 2.0**23
    digits = []
    for _ in range(DIGITS):
        digit = (value + magic) - magic
        digits.append(digit)
        value = (value - digit) * 4.0
    return digits


def place_of(row, owned, ranks):
    bits = ranks.bit_length() - 1
    far = lax.shift_right_logical(row, jnp.full_like(row, owned.bit_length() - 1))
    place = row & (owned - 1)
    for turn in range(bits):
        bit = lax.shift_right_logical(far, jnp.full_like(far, bits - 1 - turn)) & 1
        place = place + bit * (owned << turn)
    return place


def hist_kernel(
    owned, owner_hbm, codes_hbm, node_hbm, bag_hbm, resp_hbm,
    *refs,
):
    blocks = refs[:-7]
    code_ref, node_ref, owner_ref, codes_ref, bag_ref, resp_ref, sems = refs[-7:]
    nodes = owner_ref.shape[0]
    chunks = node_ref.shape[0]
    rows, feat = codes_ref.shape
    part = rows // PARTS
    copies = [
        pltpu.make_async_copy(node_hbm, node_ref, sems.at[0]),
        pltpu.make_async_copy(bag_hbm, bag_ref, sems.at[1]),
        pltpu.make_async_copy(resp_hbm, resp_ref, sems.at[2]),
        pltpu.make_async_copy(owner_hbm, owner_ref, sems.at[3]),
    ]
    for p in range(PARTS):
        span = pl.ds(p * part, part)
        copies.append(pltpu.make_async_copy(codes_hbm.at[span], codes_ref.at[span], sems.at[SMALL + p]))
    for copy in copies:
        copy.start()
    for copy in copies[:SMALL]:
        copy.wait()
    mine = lax.axis_index("rows") * owned
    node = node_ref[...]
    slot = jnp.zeros_like(node)
    for n in range(nodes):
        slot = jnp.where(node == n, owner_ref[n], slot)
    slot = slot ^ mine
    bag = bag_ref[...]
    weight = bag.astype(jnp.float32)
    grad = weight * resp_ref[...].astype(jnp.float32)
    top = jnp.max(jnp.max(jnp.abs(grad), axis=1, keepdims=True), axis=0, keepdims=True)
    scale, inverse = power_of_two_scale(top)
    values = [(bag & 1).astype(jnp.float32), (bag >> 1).astype(jnp.float32)] + digits_of(grad * scale)
    row = place_of(lax.broadcasted_iota(jnp.int32, (nodes, LANES), 0), owned, nodes // owned)
    columns = []
    for i in range(chunks):
        hit = slot[i : i + 1, :] == row
        picked = [jnp.where(hit, v[i : i + 1, :], 0.0) for v in values]
        columns.append(jnp.concatenate(picked, axis=0).astype(F8))
    picks = jnp.concatenate(columns, axis=1)
    for p in range(PARTS):
        copies[SMALL + p].wait()
        code_ref[p * part : (p + 1) * part, :] = codes_ref[p * part : (p + 1) * part, :].astype(jnp.int8)
    one, zero = jnp.asarray(1, F8), jnp.asarray(0, F8)
    for b in range(0, BINS, 2):
        code = code_ref[...]
        masks = [jnp.where(code <= jnp.asarray(b + j, jnp.int8), one, zero) for j in range(2)]
        sums = jnp.dot(picks, jnp.concatenate(masks, axis=1), preferred_element_type=jnp.float32)
        bags = sums[:nodes] + 2.0 * sums[nodes : 2 * nodes]
        grads = sums[(DIGITS + 1) * nodes :]
        for d in range(DIGITS, 1, -1):
            grads = grads * 0.25 + sums[d * nodes : (d + 1) * nodes]
        grads = grads * inverse
        for j in range(2):
            for at, table in ((b + j, bags), (BINS + b + j, grads)):
                piece = table[:, j * feat : (j + 1) * feat]
                size = nodes // len(blocks)
                for k, block in enumerate(blocks):
                    block[:, at, :] = piece[k * size : (k + 1) * size]


def flags_kernel(feature_ref, bin_ref, codes_ref, node_ref, out_ref):
    nodes = feature_ref.shape[0]
    chunks = node_ref.shape[0]
    feat = codes_ref.shape[1]
    base = lax.axis_index("feat") * feat
    lane = lax.broadcasted_iota(jnp.int32, (nodes, feat), 1)
    row = lax.broadcasted_iota(jnp.int32, (nodes, feat), 0)
    want = jnp.zeros((nodes, feat), jnp.int32)
    for n in range(nodes):
        want = jnp.where(row == n, feature_ref[n] - base, want)
    choose = (want == lane).astype(jnp.float32).astype(jnp.bfloat16)
    codes = codes_ref[...].astype(jnp.bfloat16)
    code = lax.dot_general(choose, codes, (((1,), (1,)), ((), ())), preferred_element_type=jnp.float32)
    row = lax.broadcasted_iota(jnp.int32, (nodes, LANES), 0)
    limit = jnp.zeros((nodes, LANES), jnp.int32)
    for n in range(nodes):
        limit = jnp.where(row == n, bin_ref[n], limit)
    limit = limit.astype(jnp.float32)
    for i in range(chunks):
        hit = (node_ref[i : i + 1, :] == row) & (code[:, i * LANES : (i + 1) * LANES] > limit)
        out_ref[i : i + 1, :] = jnp.sum(jnp.where(hit, 1.0, 0.0), axis=0, keepdims=True)


def gains_of(total):
    left_w, left_g = total[:BINS], total[BINS:]
    total_w, total_g = left_w[BINS - 1 :], left_g[BINS - 1 :]
    right_w = total_w - left_w
    right_g = total_g - left_g
    return (
        left_g * left_g / (left_w + LAMBDA)
        + right_g * right_g / (right_w + LAMBDA)
        - total_g * total_g / (total_w + LAMBDA)
    )


def best_kernel(count, keep_ref, *refs):
    gots, (flags_ref, out_ref, total_ref) = refs[:count], refs[count:]
    chunks = flags_ref.shape[0]
    out_ref[:chunks, :] = flags_ref[...]
    total = keep_ref[...]
    for got in gots:
        total = total + got[...]
    total_ref[...] = total
    for s in range(total_ref.shape[0]):
        gains = gains_of(total_ref[s])
        top = jnp.max(jnp.max(gains, axis=0, keepdims=True), axis=1, keepdims=True)
        out_ref[chunks + s : chunks + s + 1, :] = jnp.broadcast_to(top, (1, LANES))


def gains_kernel(total_ref, out_ref, turn_ref):
    feat = total_ref.shape[2]
    group = LANES // BINS
    for s in range(total_ref.shape[0]):
        turn_ref[...] = gains_of(total_ref[s]).T
        parts = [turn_ref[pl.ds(j, feat // group, stride=group), :] for j in range(group)]
        out_ref[s] = jnp.concatenate(parts, axis=1)


def last_kernel(node_ref, *refs):
    parts, (best_ref, child_ref) = refs[:-2], refs[-2:]
    chunks = node_ref.shape[0]
    both = functools.reduce(jnp.maximum, (part[...] for part in parts))
    child_ref[...] = 2 * node_ref[...] + (both[:chunks] > 0.5).astype(jnp.int32)
    best_ref[...] = both[chunks : chunks + best_ref.shape[0], :1]


def call(kernel, out, in_specs, out_specs, *args, scratch=(), limit=2):
    return pl.pallas_call(
        kernel,
        out_shape=out,
        in_specs=in_specs,
        out_specs=out_specs,
        scratch_shapes=scratch,
        compiler_params=pltpu.CompilerParams(vmem_limit_bytes=limit << 20),
    )(*args)


def in_hbm(value):
    return pltpu.with_memory_space_constraint(value, pltpu.HBM)


def swap(value, axis, distance):
    return lax.ppermute(value, axis, [(i, i ^ distance) for i in range(lax.axis_size(axis))])


def stages_of(ranks):
    bits = ranks.bit_length() - 1
    first = min(FIRST, bits)
    return [range(first)] + [range(t, min(t + NEXT, bits)) for t in range(first, bits, NEXT)]


def exchange(blocks, turns):
    gots = []
    for k in ORDER:
        if k < len(blocks):
            gots.append(swap(blocks[k], "rows", sum(1 << t for t in turns if k >> (turns[-1] - t) & 1)))
    return blocks[0], gots


def per_device(codes, node_ids, bag, response, owner_slot, chosen_feature, chosen_bin):
    rows_dev, feat_dev = codes.shape
    nodes = owner_slot.shape[0]
    ranks = lax.axis_size("rows")
    groups = lax.axis_size("feat")
    owned = nodes // ranks
    chunks = rows_dev // LANES
    fold = lambda a: a.reshape(chunks, LANES)
    f32 = lambda *shape: jax.ShapeDtypeStruct(shape, jnp.float32)
    stages = stages_of(ranks)
    parts = 1 << len(stages[0])
    *blocks, codes, node = call(
        functools.partial(hist_kernel, owned),
        (
            *[f32(nodes // parts, 2 * BINS, feat_dev)] * parts,
            jax.ShapeDtypeStruct((rows_dev, feat_dev), jnp.int8),
            jax.ShapeDtypeStruct((chunks, LANES), jnp.int32),
        ),
        [HBM] * 5,
        (VMEM,) * (2 + parts),
        *map(in_hbm, (owner_slot, codes, fold(node_ids), fold(bag), fold(response))),
        scratch=[
            pltpu.SMEM((nodes,), jnp.int32),
            pltpu.VMEM((rows_dev, feat_dev), jnp.int32),
            pltpu.VMEM((chunks, LANES), jnp.int32),
            pltpu.VMEM((chunks, LANES), jnp.bfloat16),
            pltpu.SemaphoreType.DMA((SMALL + PARTS,)),
        ],
        limit=6 + nodes // 4,
    )
    keep, gots = exchange(blocks, stages[0])
    flags = call(
        flags_kernel, f32(chunks, LANES), [SMEM] * 2 + [VMEM] * 2, VMEM,
        chosen_feature, chosen_bin, codes, node, limit=8,
    )
    keep, flags = lax.optimization_barrier((keep, flags))
    for turns in stages[1:]:
        total = sum(gots, keep)
        size = total.shape[0] >> len(turns)
        keep, gots = exchange([total[k * size : (k + 1) * size] for k in range(1 << len(turns))], turns)
    pad = -(-owned // 8) * 8
    payload, total = call(
        functools.partial(best_kernel, len(gots)),
        (f32(chunks + pad, LANES), f32(owned, 2 * BINS, feat_dev)),
        [VMEM] * (2 + len(gots)), (VMEM, VMEM), keep, *gots, flags,
    )
    parts = [payload]
    for k in FEATS[: groups - 1] + tuple(range(4, groups)):
        parts.append(swap(payload, "feat", k))
    gains = call(
        gains_kernel, f32(owned, feat_dev * BINS // LANES, LANES), [VMEM], VMEM, total,
        scratch=[pltpu.VMEM((feat_dev, BINS), jnp.float32)],
    )
    best, child = call(
        last_kernel,
        (f32(owned, 1), jax.ShapeDtypeStruct((chunks, LANES), jnp.int32)),
        [VMEM] * (1 + groups),
        (VMEM, VMEM),
        node, *parts,
    )
    return gains.reshape(owned, feat_dev * BINS), best.reshape(owned), child.reshape(rows_dev)


def solution(mesh):
    in_specs = (P("rows", "feat"), P("rows"), P("rows"), P("rows"), P(), P(), P())
    out_specs = (P("rows", "feat"), P("rows"), P("rows"))
    return jax.shard_map(
        per_device, mesh=mesh, in_specs=in_specs, out_specs=out_specs, check_vma=False
    )
```

```python
import functools

import jax
import jax.numpy as jnp
from jax import lax
from jax.experimental import pallas as pl
from jax.experimental.pallas import tpu as pltpu
from jax.sharding import PartitionSpec as P

BINS = 32
LAMBDA = 1.0
LANES = 128
F8 = jnp.float8_e4m3fn
VMEM = pl.BlockSpec(memory_space=pltpu.VMEM)
HBM = pl.BlockSpec(memory_space=pltpu.HBM)
SMEM = pl.BlockSpec(memory_space=pltpu.SMEM)

DIGITS = 10
FIRST, NEXT = 2, 1
ORDER = (3, 1, 2)
FEATS = (1, 2, 3)
PARTS = 4
EARLY = 1
SMALL = 4


def power_of_two_scale(top):
    top = top * 2.0**-4
    scale, inverse = jnp.full_like(top, 2.0**-4), jnp.full_like(top, 2.0**4)
    for step in (64, 32, 16, 8, 4, 2, 1):
        low = top < 2.0 ** (1 - step)
        top = jnp.where(low, top * 2.0**step, top)
        scale = jnp.where(low, scale * 2.0**step, scale)
        inverse = jnp.where(low, inverse * 2.0**-step, inverse)
    return scale, inverse


def digits_of(value):
    magic = 1.5 * 2.0**23
    digits = []
    for _ in range(DIGITS):
        digit = (value + magic) - magic
        digits.append(digit)
        value = (value - digit) * 4.0
    return digits


def place_of(row, owned, ranks):
    bits = ranks.bit_length() - 1
    far = lax.shift_right_logical(row, jnp.full_like(row, owned.bit_length() - 1))
    place = row & (owned - 1)
    for turn in range(bits):
        bit = lax.shift_right_logical(far, jnp.full_like(far, bits - 1 - turn)) & 1
        place = place + bit * (owned << turn)
    return place


def hist_kernel(
    owned, owner_hbm, codes_hbm, node_hbm, bag_hbm, resp_hbm,
    *refs,
):
    blocks = refs[:-8]
    code_ref, node_ref, owner_ref, codes_ref, bag_ref, resp_ref, sums_ref, sems = refs[-8:]
    nodes = owner_ref.shape[0]
    chunks = node_ref.shape[0]
    rows, feat = codes_ref.shape
    part = rows // PARTS
    copies = [
        pltpu.make_async_copy(node_hbm, node_ref, sems.at[0]),
        pltpu.make_async_copy(bag_hbm, bag_ref, sems.at[1]),
        pltpu.make_async_copy(resp_hbm, resp_ref, sems.at[2]),
        pltpu.make_async_copy(owner_hbm, owner_ref, sems.at[3]),
    ]
    for p in range(PARTS):
        span = pl.ds(p * part, part)
        copies.append(pltpu.make_async_copy(codes_hbm.at[span], codes_ref.at[span], sems.at[SMALL + p]))
    for copy in copies:
        copy.start()
    for copy in copies[:SMALL]:
        copy.wait()
    mine = lax.axis_index("rows") * owned
    node = node_ref[...]
    slot = jnp.zeros_like(node)
    for n in range(nodes):
        slot = jnp.where(node == n, owner_ref[n], slot)
    slot = slot ^ mine
    bag = bag_ref[...]
    weight = bag.astype(jnp.float32)
    grad = weight * resp_ref[...].astype(jnp.float32)
    top = jnp.max(jnp.max(jnp.abs(grad), axis=1, keepdims=True), axis=0, keepdims=True)
    scale, inverse = power_of_two_scale(top)
    values = [(bag & 1).astype(jnp.float32), (bag >> 1).astype(jnp.float32)] + digits_of(grad * scale)
    row = place_of(lax.broadcasted_iota(jnp.int32, (nodes, LANES), 0), owned, nodes // owned)
    columns = []
    for i in range(chunks):
        hit = slot[i : i + 1, :] == row
        picked = [jnp.where(hit, v[i : i + 1, :], 0.0) for v in values]
        columns.append(jnp.concatenate(picked, axis=0).astype(F8))
    picks = jnp.concatenate(columns, axis=1)
    one, zero = jnp.asarray(1, F8), jnp.asarray(0, F8)

    def sums_of(b, first, last):
        code = code_ref[first:last, :]
        masks = [jnp.where(code <= jnp.asarray(b + j, jnp.int8), one, zero) for j in range(2)]
        return jnp.dot(picks[:, first:last], jnp.concatenate(masks, axis=1), preferred_element_type=jnp.float32)

    def take(p):
        copies[SMALL + p].wait()
        code_ref[p * part : (p + 1) * part, :] = codes_ref[p * part : (p + 1) * part, :].astype(jnp.int8)

    early = EARLY * part
    for p in range(EARLY):
        take(p)
    for b in range(0, BINS, 2):
        sums_ref[:, b * feat : (b + 2) * feat] = sums_of(b, 0, early)
    for p in range(EARLY, PARTS):
        take(p)
    for b in range(0, BINS, 2):
        sums = sums_ref[:, b * feat : (b + 2) * feat] + sums_of(b, early, rows)
        bags = sums[:nodes] + 2.0 * sums[nodes : 2 * nodes]
        grads = sums[(DIGITS + 1) * nodes :]
        for d in range(DIGITS, 1, -1):
            grads = grads * 0.25 + sums[d * nodes : (d + 1) * nodes]
        grads = grads * inverse
        for j in range(2):
            for at, table in ((b + j, bags), (BINS + b + j, grads)):
                piece = table[:, j * feat : (j + 1) * feat]
                size = nodes // len(blocks)
                for k, block in enumerate(blocks):
                    block[:, at, :] = piece[k * size : (k + 1) * size]


def flags_kernel(feature_ref, bin_ref, codes_ref, node_ref, out_ref):
    nodes = feature_ref.shape[0]
    chunks = node_ref.shape[0]
    feat = codes_ref.shape[1]
    base = lax.axis_index("feat") * feat
    lane = lax.broadcasted_iota(jnp.int32, (nodes, feat), 1)
    row = lax.broadcasted_iota(jnp.int32, (nodes, feat), 0)
    want = jnp.zeros((nodes, feat), jnp.int32)
    for n in range(nodes):
        want = jnp.where(row == n, feature_ref[n] - base, want)
    choose = (want == lane).astype(jnp.float32).astype(jnp.bfloat16)
    codes = codes_ref[...].astype(jnp.bfloat16)
    code = lax.dot_general(choose, codes, (((1,), (1,)), ((), ())), preferred_element_type=jnp.float32)
    row = lax.broadcasted_iota(jnp.int32, (nodes, LANES), 0)
    limit = jnp.zeros((nodes, LANES), jnp.int32)
    for n in range(nodes):
        limit = jnp.where(row == n, bin_ref[n], limit)
    limit = limit.astype(jnp.float32)
    for i in range(chunks):
        hit = (node_ref[i : i + 1, :] == row) & (code[:, i * LANES : (i + 1) * LANES] > limit)
        out_ref[i : i + 1, :] = jnp.sum(jnp.where(hit, 1.0, 0.0), axis=0, keepdims=True)


def gains_of(total):
    left_w, left_g = total[:BINS], total[BINS:]
    total_w, total_g = left_w[BINS - 1 :], left_g[BINS - 1 :]
    right_w = total_w - left_w
    right_g = total_g - left_g
    return (
        left_g * left_g / (left_w + LAMBDA)
        + right_g * right_g / (right_w + LAMBDA)
        - total_g * total_g / (total_w + LAMBDA)
    )


def best_kernel(count, keep_ref, *refs):
    gots, (flags_ref, out_ref, total_ref) = refs[:count], refs[count:]
    chunks = flags_ref.shape[0]
    out_ref[:chunks, :] = flags_ref[...]
    total = keep_ref[...]
    for got in gots:
        total = total + got[...]
    total_ref[...] = total
    for s in range(total_ref.shape[0]):
        gains = gains_of(total_ref[s])
        top = jnp.max(jnp.max(gains, axis=0, keepdims=True), axis=1, keepdims=True)
        out_ref[chunks + s : chunks + s + 1, :] = jnp.broadcast_to(top, (1, LANES))


def gains_kernel(total_ref, out_ref, turn_ref):
    feat = total_ref.shape[2]
    group = LANES // BINS
    for s in range(total_ref.shape[0]):
        turn_ref[...] = gains_of(total_ref[s]).T
        parts = [turn_ref[pl.ds(j, feat // group, stride=group), :] for j in range(group)]
        out_ref[s] = jnp.concatenate(parts, axis=1)


def last_kernel(node_ref, *refs):
    parts, (best_ref, child_ref) = refs[:-2], refs[-2:]
    chunks = node_ref.shape[0]
    both = functools.reduce(jnp.maximum, (part[...] for part in parts))
    child_ref[...] = 2 * node_ref[...] + (both[:chunks] > 0.5).astype(jnp.int32)
    best_ref[...] = both[chunks : chunks + best_ref.shape[0], :1]


def call(kernel, out, in_specs, out_specs, *args, scratch=(), limit=2):
    return pl.pallas_call(
        kernel,
        out_shape=out,
        in_specs=in_specs,
        out_specs=out_specs,
        scratch_shapes=scratch,
        compiler_params=pltpu.CompilerParams(vmem_limit_bytes=limit << 20),
    )(*args)


def in_hbm(value):
    return pltpu.with_memory_space_constraint(value, pltpu.HBM)


def swap(value, axis, distance):
    return lax.ppermute(value, axis, [(i, i ^ distance) for i in range(lax.axis_size(axis))])


def stages_of(ranks):
    bits = ranks.bit_length() - 1
    first = min(FIRST, bits)
    return [range(first)] + [range(t, min(t + NEXT, bits)) for t in range(first, bits, NEXT)]


def exchange(blocks, turns):
    gots = []
    for k in ORDER:
        if k < len(blocks):
            gots.append(swap(blocks[k], "rows", sum(1 << t for t in turns if k >> (turns[-1] - t) & 1)))
    return blocks[0], gots


def per_device(codes, node_ids, bag, response, owner_slot, chosen_feature, chosen_bin):
    rows_dev, feat_dev = codes.shape
    nodes = owner_slot.shape[0]
    ranks = lax.axis_size("rows")
    groups = lax.axis_size("feat")
    owned = nodes // ranks
    chunks = rows_dev // LANES
    fold = lambda a: a.reshape(chunks, LANES)
    f32 = lambda *shape: jax.ShapeDtypeStruct(shape, jnp.float32)
    stages = stages_of(ranks)
    parts = 1 << len(stages[0])
    *blocks, codes, node = call(
        functools.partial(hist_kernel, owned),
        (
            *[f32(nodes // parts, 2 * BINS, feat_dev)] * parts,
            jax.ShapeDtypeStruct((rows_dev, feat_dev), jnp.int8),
            jax.ShapeDtypeStruct((chunks, LANES), jnp.int32),
        ),
        [HBM] * 5,
        (VMEM,) * (2 + parts),
        *map(in_hbm, (owner_slot, codes, fold(node_ids), fold(bag), fold(response))),
        scratch=[
            pltpu.SMEM((nodes,), jnp.int32),
            pltpu.VMEM((rows_dev, feat_dev), jnp.int32),
            pltpu.VMEM((chunks, LANES), jnp.int32),
            pltpu.VMEM((chunks, LANES), jnp.bfloat16),
            pltpu.VMEM(((DIGITS + 2) * nodes, BINS * feat_dev), jnp.float32),
            pltpu.SemaphoreType.DMA((SMALL + PARTS,)),
        ],
        limit=8 + nodes * 3 // 8,
    )
    keep, gots = exchange(blocks, stages[0])
    for turns in stages[1:]:
        total = sum(gots, keep)
        total, codes = lax.optimization_barrier((total, codes))
        size = total.shape[0] >> len(turns)
        keep, gots = exchange([total[k * size : (k + 1) * size] for k in range(1 << len(turns))], turns)
    flags = call(
        flags_kernel, f32(chunks, LANES), [SMEM] * 2 + [VMEM] * 2, VMEM,
        in_hbm(chosen_feature), in_hbm(chosen_bin), codes, node, limit=8,
    )
    pad = -(-owned // 8) * 8
    payload, total = call(
        functools.partial(best_kernel, len(gots)),
        (f32(chunks + pad, LANES), f32(owned, 2 * BINS, feat_dev)),
        [VMEM] * (2 + len(gots)), (VMEM, VMEM), keep, *gots, flags,
    )
    parts = [payload]
    for k in FEATS[: groups - 1] + tuple(range(4, groups)):
        parts.append(swap(payload, "feat", k))
    gains = call(
        gains_kernel, f32(owned, feat_dev * BINS // LANES, LANES), [VMEM], VMEM, total,
        scratch=[pltpu.VMEM((feat_dev, BINS), jnp.float32)],
    )
    best, child = call(
        last_kernel,
        (f32(owned, 1), jax.ShapeDtypeStruct((chunks, LANES), jnp.int32)),
        [VMEM] * (1 + groups),
        (VMEM, VMEM),
        node, *parts,
    )
    return gains.reshape(owned, feat_dev * BINS), best.reshape(owned), child.reshape(rows_dev)


def solution(mesh):
    in_specs = (P("rows", "feat"), P("rows"), P("rows"), P("rows"), P(), P(), P())
    out_specs = (P("rows", "feat"), P("rows"), P("rows"))
    return jax.shard_map(
        per_device, mesh=mesh, in_specs=in_specs, out_specs=out_specs, check_vma=False
    )
```

```python
import functools

import jax
import jax.numpy as jnp
from jax import lax
from jax.experimental import pallas as pl
from jax.experimental.pallas import tpu as pltpu
from jax.sharding import PartitionSpec as P

BINS = 32
LAMBDA = 1.0
LANES = 128
F8 = jnp.float8_e4m3fn
VMEM = pl.BlockSpec(memory_space=pltpu.VMEM)
HBM = pl.BlockSpec(memory_space=pltpu.HBM)
SMEM = pl.BlockSpec(memory_space=pltpu.SMEM)

DIGITS = 10
FIRST, NEXT = 2, 1
ORDER = (3, 1, 2)
FEATS = (1, 2, 3)
TURNED = (2, 1)
PARTS = 4
EARLY = 1
SMALL = 4


def power_of_two_scale(top):
    top = top * 2.0**-4
    scale, inverse = jnp.full_like(top, 2.0**-4), jnp.full_like(top, 2.0**4)
    for step in (64, 32, 16, 8, 4, 2, 1):
        low = top < 2.0 ** (1 - step)
        top = jnp.where(low, top * 2.0**step, top)
        scale = jnp.where(low, scale * 2.0**step, scale)
        inverse = jnp.where(low, inverse * 2.0**-step, inverse)
    return scale, inverse


def digits_of(value):
    magic = 1.5 * 2.0**23
    digits = []
    for _ in range(DIGITS):
        digit = (value + magic) - magic
        digits.append(digit)
        value = (value - digit) * 4.0
    return digits


def distance(turn, odd):
    return TURNED[turn] if odd and turn < len(TURNED) else 1 << turn


def place_of(row, owned, ranks, odd):
    bits = ranks.bit_length() - 1
    far = lax.shift_right_logical(row, jnp.full_like(row, owned.bit_length() - 1))
    place = row & (owned - 1)
    for turn in range(bits):
        bit = lax.shift_right_logical(far, jnp.full_like(far, bits - 1 - turn)) & 1
        place = place ^ (bit * (owned * jnp.where(odd, distance(turn, True), distance(turn, False))))
    return place


def hist_kernel(
    owned, owner_hbm, codes_hbm, node_hbm, bag_hbm, resp_hbm,
    *refs,
):
    blocks = refs[:-8]
    code_ref, node_ref, owner_ref, codes_ref, bag_ref, resp_ref, sums_ref, sems = refs[-8:]
    nodes = owner_ref.shape[0]
    chunks = node_ref.shape[0]
    rows, feat = codes_ref.shape
    part = rows // PARTS
    copies = [
        pltpu.make_async_copy(node_hbm, node_ref, sems.at[0]),
        pltpu.make_async_copy(bag_hbm, bag_ref, sems.at[1]),
        pltpu.make_async_copy(resp_hbm, resp_ref, sems.at[2]),
        pltpu.make_async_copy(owner_hbm, owner_ref, sems.at[3]),
    ]
    for p in range(PARTS):
        span = pl.ds(p * part, part)
        copies.append(pltpu.make_async_copy(codes_hbm.at[span], codes_ref.at[span], sems.at[SMALL + p]))
    for copy in copies:
        copy.start()
    for copy in copies[:SMALL]:
        copy.wait()
    mine = lax.axis_index("rows") * owned
    node = node_ref[...]
    slot = jnp.zeros_like(node)
    for n in range(nodes):
        slot = jnp.where(node == n, owner_ref[n], slot)
    slot = slot ^ mine
    bag = bag_ref[...]
    weight = bag.astype(jnp.float32)
    grad = weight * resp_ref[...].astype(jnp.float32)
    top = jnp.max(jnp.max(jnp.abs(grad), axis=1, keepdims=True), axis=0, keepdims=True)
    scale, inverse = power_of_two_scale(top)
    values = [(bag & 1).astype(jnp.float32), (bag >> 1).astype(jnp.float32)] + digits_of(grad * scale)
    row = place_of(lax.broadcasted_iota(jnp.int32, (nodes, LANES), 0), owned, nodes // owned, lax.axis_index("feat") & 1 == 1)
    columns = []
    for i in range(chunks):
        hit = slot[i : i + 1, :] == row
        picked = [jnp.where(hit, v[i : i + 1, :], 0.0) for v in values]
        columns.append(jnp.concatenate(picked, axis=0).astype(F8))
    picks = jnp.concatenate(columns, axis=1)
    one, zero = jnp.asarray(1, F8), jnp.asarray(0, F8)

    def sums_of(b, first, last):
        code = code_ref[first:last, :]
        masks = [jnp.where(code <= jnp.asarray(b + j, jnp.int8), one, zero) for j in range(2)]
        return jnp.dot(picks[:, first:last], jnp.concatenate(masks, axis=1), preferred_element_type=jnp.float32)

    def take(p):
        copies[SMALL + p].wait()
        code_ref[p * part : (p + 1) * part, :] = codes_ref[p * part : (p + 1) * part, :].astype(jnp.int8)

    early = EARLY * part
    for p in range(EARLY):
        take(p)
    for b in range(0, BINS, 2):
        sums_ref[:, b * feat : (b + 2) * feat] = sums_of(b, 0, early)
    for p in range(EARLY, PARTS):
        take(p)
    for b in range(0, BINS, 2):
        sums = sums_ref[:, b * feat : (b + 2) * feat] + sums_of(b, early, rows)
        bags = sums[:nodes] + 2.0 * sums[nodes : 2 * nodes]
        grads = sums[(DIGITS + 1) * nodes :]
        for d in range(DIGITS, 1, -1):
            grads = grads * 0.25 + sums[d * nodes : (d + 1) * nodes]
        grads = grads * inverse
        for j in range(2):
            for at, table in ((b + j, bags), (BINS + b + j, grads)):
                piece = table[:, j * feat : (j + 1) * feat]
                size = nodes // len(blocks)
                for k, block in enumerate(blocks):
                    block[:, at, :] = piece[k * size : (k + 1) * size]


def flags_kernel(feature_ref, bin_ref, codes_ref, node_ref, out_ref):
    nodes = feature_ref.shape[0]
    chunks = node_ref.shape[0]
    feat = codes_ref.shape[1]
    base = lax.axis_index("feat") * feat
    lane = lax.broadcasted_iota(jnp.int32, (nodes, feat), 1)
    row = lax.broadcasted_iota(jnp.int32, (nodes, feat), 0)
    want = jnp.zeros((nodes, feat), jnp.int32)
    for n in range(nodes):
        want = jnp.where(row == n, feature_ref[n] - base, want)
    choose = (want == lane).astype(jnp.float32).astype(jnp.bfloat16)
    codes = codes_ref[...].astype(jnp.bfloat16)
    code = lax.dot_general(choose, codes, (((1,), (1,)), ((), ())), preferred_element_type=jnp.float32)
    row = lax.broadcasted_iota(jnp.int32, (nodes, LANES), 0)
    limit = jnp.zeros((nodes, LANES), jnp.int32)
    for n in range(nodes):
        limit = jnp.where(row == n, bin_ref[n], limit)
    limit = limit.astype(jnp.float32)
    for i in range(chunks):
        hit = (node_ref[i : i + 1, :] == row) & (code[:, i * LANES : (i + 1) * LANES] > limit)
        out_ref[i : i + 1, :] = jnp.sum(jnp.where(hit, 1.0, 0.0), axis=0, keepdims=True)


def gains_of(total):
    left_w, left_g = total[:BINS], total[BINS:]
    total_w, total_g = left_w[BINS - 1 :], left_g[BINS - 1 :]
    right_w = total_w - left_w
    right_g = total_g - left_g
    return (
        left_g * left_g / (left_w + LAMBDA)
        + right_g * right_g / (right_w + LAMBDA)
        - total_g * total_g / (total_w + LAMBDA)
    )


def best_kernel(count, keep_ref, *refs):
    gots, (flags_ref, out_ref, total_ref) = refs[:count], refs[count:]
    chunks = flags_ref.shape[0]
    out_ref[:chunks, :] = flags_ref[...]
    total = keep_ref[...]
    for got in gots:
        total = total + got[...]
    total_ref[...] = total
    for s in range(total_ref.shape[0]):
        gains = gains_of(total_ref[s])
        top = jnp.max(jnp.max(gains, axis=0, keepdims=True), axis=1, keepdims=True)
        out_ref[chunks + s : chunks + s + 1, :] = jnp.broadcast_to(top, (1, LANES))


def gains_kernel(total_ref, out_ref, turn_ref):
    feat = total_ref.shape[2]
    group = LANES // BINS
    for s in range(total_ref.shape[0]):
        turn_ref[...] = gains_of(total_ref[s]).T
        parts = [turn_ref[pl.ds(j, feat // group, stride=group), :] for j in range(group)]
        out_ref[s] = jnp.concatenate(parts, axis=1)


def last_kernel(node_ref, *refs):
    parts, (best_ref, child_ref) = refs[:-2], refs[-2:]
    chunks = node_ref.shape[0]
    both = functools.reduce(jnp.maximum, (part[...] for part in parts))
    child_ref[...] = 2 * node_ref[...] + (both[:chunks] > 0.5).astype(jnp.int32)
    best_ref[...] = both[chunks : chunks + best_ref.shape[0], :1]


def call(kernel, out, in_specs, out_specs, *args, scratch=(), limit=2):
    return pl.pallas_call(
        kernel,
        out_shape=out,
        in_specs=in_specs,
        out_specs=out_specs,
        scratch_shapes=scratch,
        compiler_params=pltpu.CompilerParams(vmem_limit_bytes=limit << 20),
    )(*args)


def in_hbm(value):
    return pltpu.with_memory_space_constraint(value, pltpu.HBM)


def swap(value, axis, distance):
    return lax.ppermute(value, axis, [(i, i ^ distance) for i in range(lax.axis_size(axis))])


def swap_rows(value, turns):
    ranks, groups = lax.axis_size("rows"), lax.axis_size("feat")
    pairs = []
    for row in range(ranks):
        for feat in range(groups):
            partner = row
            for turn in turns:
                partner ^= distance(turn, feat % 2 == 1)
            pairs.append((row * groups + feat, partner * groups + feat))
    return lax.ppermute(value, ("rows", "feat"), pairs)


def stages_of(ranks):
    bits = ranks.bit_length() - 1
    first = min(FIRST, bits)
    return [range(first)] + [range(t, min(t + NEXT, bits)) for t in range(first, bits, NEXT)]


def exchange(blocks, turns):
    gots = []
    for k in ORDER:
        if k < len(blocks):
            gots.append(swap_rows(blocks[k], [t for t in turns if k >> (turns[-1] - t) & 1]))
    return blocks[0], gots


def per_device(codes, node_ids, bag, response, owner_slot, chosen_feature, chosen_bin):
    rows_dev, feat_dev = codes.shape
    nodes = owner_slot.shape[0]
    ranks = lax.axis_size("rows")
    groups = lax.axis_size("feat")
    owned = nodes // ranks
    chunks = rows_dev // LANES
    fold = lambda a: a.reshape(chunks, LANES)
    f32 = lambda *shape: jax.ShapeDtypeStruct(shape, jnp.float32)
    stages = stages_of(ranks)
    parts = 1 << len(stages[0])
    *blocks, codes, node = call(
        functools.partial(hist_kernel, owned),
        (
            *[f32(nodes // parts, 2 * BINS, feat_dev)] * parts,
            jax.ShapeDtypeStruct((rows_dev, feat_dev), jnp.int8),
            jax.ShapeDtypeStruct((chunks, LANES), jnp.int32),
        ),
        [HBM] * 5,
        (VMEM,) * (2 + parts),
        *map(in_hbm, (owner_slot, codes, fold(node_ids), fold(bag), fold(response))),
        scratch=[
            pltpu.SMEM((nodes,), jnp.int32),
            pltpu.VMEM((rows_dev, feat_dev), jnp.int32),
            pltpu.VMEM((chunks, LANES), jnp.int32),
            pltpu.VMEM((chunks, LANES), jnp.bfloat16),
            pltpu.VMEM(((DIGITS + 2) * nodes, BINS * feat_dev), jnp.float32),
            pltpu.SemaphoreType.DMA((SMALL + PARTS,)),
        ],
        limit=8 + nodes * 3 // 8,
    )
    keep, gots = exchange(blocks, stages[0])
    for turns in stages[1:]:
        total = sum(gots, keep)
        total, codes = lax.optimization_barrier((total, codes))
        size = total.shape[0] >> len(turns)
        keep, gots = exchange([total[k * size : (k + 1) * size] for k in range(1 << len(turns))], turns)
    flags = call(
        flags_kernel, f32(chunks, LANES), [SMEM] * 2 + [VMEM] * 2, VMEM,
        in_hbm(chosen_feature), in_hbm(chosen_bin), codes, node, limit=8,
    )
    pad = -(-owned // 8) * 8
    payload, total = call(
        functools.partial(best_kernel, len(gots)),
        (f32(chunks + pad, LANES), f32(owned, 2 * BINS, feat_dev)),
        [VMEM] * (2 + len(gots)), (VMEM, VMEM), keep, *gots, flags,
    )
    parts = [payload]
    for k in FEATS[: groups - 1] + tuple(range(4, groups)):
        parts.append(swap(payload, "feat", k))
    gains = call(
        gains_kernel, f32(owned, feat_dev * BINS // LANES, LANES), [VMEM], VMEM, total,
        scratch=[pltpu.VMEM((feat_dev, BINS), jnp.float32)],
    )
    best, child = call(
        last_kernel,
        (f32(owned, 1), jax.ShapeDtypeStruct((chunks, LANES), jnp.int32)),
        [VMEM] * (1 + groups),
        (VMEM, VMEM),
        node, *parts,
    )
    return gains.reshape(owned, feat_dev * BINS), best.reshape(owned), child.reshape(rows_dev)


def solution(mesh):
    in_specs = (P("rows", "feat"), P("rows"), P("rows"), P("rows"), P(), P(), P())
    out_specs = (P("rows", "feat"), P("rows"), P("rows"))
    return jax.shard_map(
        per_device, mesh=mesh, in_specs=in_specs, out_specs=out_specs, check_vma=False
    )
```
